512 devices in a mesh: section: 8 (over y, core), dp: 64 (over x, z).
Axes of the slice: x: 4, y: 4, z: 16, core: 2. Of those that a mesh axis runs over, the one named last changes fastest.
Arguments:
- acts: bfloat16 [8, 16384, 4096], P('section', 'dp'), may hold values from -16 to 16
- cotangent: bfloat16 [16384, 4096], P('dp'), may hold values from -0.3125 to 0.3125
- weights: bfloat16 [8, 4096, 256], P('section', 'dp'), may hold values from -0.0625 to 0.0625
- doc_ids: int32 [128], P('dp'), may hold values from 0 to 1, as said below
- lang_ids: int32 [128], P('dp'), may hold values from 0 to 15
- temper: float32 [16], replicated, may hold values from 0.25 to 4
Outputs:
- grads: float32 [8, 4096, 256], P('section', 'dp')
The draws below stay inside these ranges and needn't reach their ends.
Inputs may be any that keep to these rules, and one draw needn't show every extreme that they name: `doc_ids`: within each replica's 2 entries the first is 0 and each next one is equal or larger by 1.
All inputs are finite; a program needn't handle non-finite values.
Results may differ from the reference program's by a relative error of at most 0.014.
Values may be sent and summed in bfloat16 or wider, within the bound.
A program may use at most 64 MiB of HBM per device.

```python
import math
import jax
import jax.numpy as jnp
from jax import lax

D = 4096
DH = 64
TOK_DEV = 256
UNIT = 128
LANGS = 16
SECTIONS = 8
REPLICAS = 64
TOKENS = 16384
DOC_SLOTS = 2


def draw_weights(key, part):
    shape_all = (SECTIONS, D, 4 * DH)
    values_raw = jnp.clip(jax.random.normal(key, shape_all, jnp.float32), -4.0, 4.0)
    return (values_raw * D ** (-0.5)).astype(jnp.bfloat16)


def draw_doc_ids(key, part):
    coins = jax.random.randint(key, (REPLICAS, DOC_SLOTS), 0, 4)
    lanes = jnp.arange(DOC_SLOTS, dtype=jnp.int32)[None, :]
    replica_rows = jnp.arange(REPLICAS, dtype=jnp.int32)[:, None]
    starts = (coins == 0) | (lanes == 0) | (replica_rows == 0)
    starts = starts & ((replica_rows != 1) | (lanes == 0))
    doc_numbers = jnp.cumsum(starts.astype(jnp.int32), axis=1) - 1
    return doc_numbers.reshape(-1).astype(jnp.int32)


def touch_ends(result, stream_key, low, largest):
    longest = result.shape.index(max(result.shape))
    spots = []
    for shift in (0, 1):
        where = [jax.random.randint(jax.random.fold_in(stream_key, axis), (), 0, length) for axis, length in enumerate(result.shape)]
        where[longest] = (where[longest] + shift) % result.shape[longest]
        spots.append(tuple(where))
    return result.at[spots[0]].set(low).at[spots[1]].set(largest)


def spiked(drawn, stream_key, source, target, blocks, factor):
    owner, partner = [(jnp.arange(drawn.shape[position]) // (drawn.shape[position] // blocks)).reshape([-1 if axis == position else 1 for axis in range(drawn.ndim)]) for position in (source, target)]
    chosen = jax.random.permutation(stream_key, blocks)[partner]
    strong = (owner == chosen) | (owner == (partner + blocks // 2) % blocks)
    return jnp.where(strong, factor * drawn, drawn)


def block_scale(rng, extent, pieces, least, high):
    level = 1.0
    for dim, shards_of in pieces:
        heights = jax.random.uniform(jax.random.fold_in(jax.random.fold_in(rng, 6), dim), (shards_of,), jnp.float32, least / len(pieces), high / len(pieces))
        level = level * jnp.repeat(jnp.exp(heights), extent[dim] // shards_of).reshape((-1,) + (1,) * (len(extent) - 1 - dim))
    return level


def gaussian_with(rng, dims, width, limit, pieces, heavy, held_as=jnp.bfloat16):
    array = width * jax.random.normal(rng, dims, jnp.float32)
    if pieces:
        array = array * block_scale(rng, dims, pieces, -0.22, 0.18)
    return jnp.clip(spiked(array, jax.random.fold_in(rng, 3), *heavy), -limit, limit).astype(held_as)


def setup_inputs(seed: int = 0) -> dict:
    splits = jax.random.split(jax.random.key(seed), 7)
    acts = gaussian_with(splits[0], (SECTIONS, TOKENS, D), 1.0, 16.0, ((0, 8), (1, 64)), (1, 2, 64, 4.0))
    cotangent = gaussian_with(splits[1], (TOKENS, D), 0.02, 0.3125, ((0, 64),), (0, 1, 64, 4.0))
    weights = draw_weights(jax.random.fold_in(splits[6], 71), 0)
    doc_ids = draw_doc_ids(jax.random.fold_in(splits[6], 71), 0)
    lang_ids = touch_ends(jax.random.randint(splits[4], (TOKENS // UNIT,), 0, LANGS), jax.random.fold_in(splits[4], 1), 0, LANGS - 1).astype(jnp.int32)
    temper = jnp.clip(jnp.exp(jax.random.uniform(splits[5], (LANGS,), jnp.float32, math.log(0.25), math.log(4.0))), 0.25, 4.0)
    return {"acts": acts, "cotangent": cotangent, "weights": weights, "doc_ids": doc_ids, "lang_ids": lang_ids, "temper": temper}


def layer_backward(layer_in, weight_all, grad_in, allowed):
    head_size = DH
    inputs_wide = layer_in.astype(jnp.float32)
    inv_rms = lax.rsqrt(lax.optimization_barrier(jnp.mean(inputs_wide * inputs_wide, axis=1, keepdims=True)) + 1e-05)
    normed = (inputs_wide * inv_rms).astype(jnp.bfloat16)
    w_qkv = weight_all[:, :3 * head_size]
    w_out = weight_all[:, 3 * head_size:]
    projected = jnp.dot(normed, w_qkv, preferred_element_type=jnp.float32).astype(jnp.bfloat16)
    query_rows = projected[:, :head_size]
    key_rows = projected[:, head_size:2 * head_size]
    value_rows = projected[:, 2 * head_size:]
    score_scale = head_size ** (-0.5)
    scores = jnp.dot(query_rows, key_rows.T, preferred_element_type=jnp.float32) * score_scale
    exp_terms = jnp.where(allowed, jnp.exp(scores), jnp.float32(0.0))
    attn_probs = exp_terms / lax.optimization_barrier(jnp.sum(exp_terms, axis=1, keepdims=True))
    probs_low = attn_probs.astype(jnp.bfloat16)
    attended = jnp.dot(probs_low, value_rows, preferred_element_type=jnp.float32)
    attended_low = attended.astype(jnp.bfloat16)
    out_grad = jnp.dot(grad_in, w_out, preferred_element_type=jnp.float32).astype(jnp.bfloat16)
    prob_grad = jnp.dot(out_grad, value_rows.T, preferred_element_type=jnp.float32)
    row_delta = lax.optimization_barrier(jnp.sum(out_grad.astype(jnp.float32) * attended, axis=1, keepdims=True))
    score_grad = (attn_probs * (prob_grad - row_delta) * score_scale).astype(jnp.bfloat16)
    query_grad = jnp.dot(score_grad, key_rows, preferred_element_type=jnp.float32).astype(jnp.bfloat16)
    key_grad = jnp.dot(score_grad.T, query_rows, preferred_element_type=jnp.float32).astype(jnp.bfloat16)
    value_grad = jnp.dot(probs_low.T, out_grad, preferred_element_type=jnp.float32).astype(jnp.bfloat16)
    proj_grad = jnp.concatenate([query_grad, key_grad, value_grad], axis=1)
    normed_grad = jnp.dot(proj_grad, w_qkv.T, preferred_element_type=jnp.float32)
    inv_cube = inv_rms * inv_rms * inv_rms
    input_grad = grad_in.astype(jnp.float32) + inv_rms * normed_grad - inputs_wide * inv_cube * lax.optimization_barrier(jnp.mean(normed_grad * inputs_wide, axis=1, keepdims=True))
    weight_grad = jnp.concatenate([jnp.dot(normed.T, proj_grad, preferred_element_type=jnp.float32), jnp.dot(grad_in.T, attended_low, preferred_element_type=jnp.float32)], axis=1)
    return (input_grad.astype(jnp.bfloat16), weight_grad)

def reference(acts, cotangent, weights, doc_ids, lang_ids, temper):

    def one_replica(running, replica):
        token_base = replica * TOK_DEV
        slot_base = replica * DOC_SLOTS
        layer_inputs = lax.dynamic_slice_in_dim(acts, token_base, TOK_DEV, 1)
        cot_rows = lax.dynamic_slice_in_dim(cotangent, token_base, TOK_DEV, 0)
        doc_slots = lax.dynamic_slice_in_dim(doc_ids, slot_base, DOC_SLOTS, 0)
        lang_slots = lax.dynamic_slice_in_dim(lang_ids, slot_base, DOC_SLOTS, 0)
        doc_tok = jnp.repeat(doc_slots, UNIT)
        positions = jnp.arange(TOK_DEV, dtype=jnp.int32)
        allowed = (doc_tok[:, None] == doc_tok[None, :]) & (positions[None, :] <= positions[:, None])
        tok_weight = temper[lang_slots[doc_tok]]
        grad_in = (cot_rows.astype(jnp.float32) * tok_weight[:, None]).astype(jnp.bfloat16)
        layer_grads = []
        for layer_idx in reversed(range(SECTIONS)):
            grad_in, weight_grad = layer_backward(layer_inputs[layer_idx], weights[layer_idx], grad_in, allowed)
            layer_grads.append(weight_grad)
        stacked = jnp.stack(layer_grads[::-1])
        return (running + stacked, None)
    start_sum = jnp.zeros((SECTIONS, D, 4 * DH), jnp.float32)
    totals, unused = lax.scan(one_replica, start_sum, jnp.arange(REPLICAS, dtype=jnp.int32))
    return totals
```

```python
from functools import partial

import jax
import jax.numpy as jnp
from jax import lax
from jax.experimental import pallas as pl
from jax.experimental.pallas import tpu as pltpu
from jax.sharding import PartitionSpec as P

DH = 64
MESH = pl.DeviceIdType.MESH
NX = 4
NZ = 16
VMEM_LIMIT = 56 << 20


def place():
    me = lax.axis_index("dp")
    return me // NZ, lax.rem(me, NZ)


def dp_of(x, z):
    return lax.rem(x + NX, NX) * NZ + lax.rem(z + NZ, NZ)


def greet(x, z):
    barrier = pltpu.get_barrier_semaphore()
    others = [dp_of(x, z + 1), dp_of(x, z - 1)] + [dp_of(x + k, z) for k in range(1, NX)]
    for other in others:
        pl.semaphore_signal(barrier, inc=1, device_id={"dp": other}, device_id_type=MESH)
    pl.semaphore_wait(barrier, len(others))


def gather_kernel(w_ref, out_ref, send_z, send_x, recv, own_sem):
    x, z = place()
    rows = w_ref.shape[0]

    def block(xx, zz):
        return pl.ds(pl.multiple_of(dp_of(xx, zz) * rows, rows), rows)

    greet(x, z)
    own = pltpu.make_async_copy(w_ref, out_ref.at[block(x, z)], own_sem)
    own.start()
    sends = []

    def pass_on(src, zz, target, send_sem):
        copy = pltpu.make_async_remote_copy(
            src_ref=src,
            dst_ref=out_ref.at[block(x, zz)],
            send_sem=send_sem,
            recv_sem=recv.at[dp_of(x, zz)],
            device_id={"dp": target},
            device_id_type=MESH,
        )
        copy.start()
        sends.append(copy)

    def arrived(xx, zz):
        pltpu.make_async_copy(out_ref.at[block(xx, zz)], out_ref.at[block(xx, zz)], recv.at[dp_of(xx, zz)]).wait()

    pass_on(w_ref, z, dp_of(x, z + 1), send_z.at[0])
    pass_on(w_ref, z, dp_of(x, z - 1), send_z.at[1])
    for k in range(1, NX):
        pass_on(w_ref, z, dp_of(x + k, z), send_x.at[0, k - 1])
    half = NZ // 2
    for step in range(1, half + 1):
        for way, reach in ((1, half), (-1, half - 1)):
            if step > reach:
                continue
            zz = z - way * step
            arrived(x, zz)
            src = out_ref.at[block(x, zz)]
            if step < reach:
                pass_on(src, zz, dp_of(x, z + way), send_z.at[2 * step + (way < 0)])
            for k in range(1, NX):
                pass_on(src, zz, dp_of(x + k, z), send_x.at[2 * step - 1 + (way < 0), k - 1])
    for k in range(1, NX):
        for zz in range(NZ):
            arrived(x + k, z + zz)
    for copy in sends:
        copy.wait_send()
    own.wait()


def gather_weights(w):
    rows, cols = w.shape
    return pl.pallas_call(
        gather_kernel,
        out_shape=jax.ShapeDtypeStruct((rows * NX * NZ, cols), w.dtype),
        in_specs=[pl.BlockSpec(memory_space=pltpu.VMEM)],
        out_specs=pl.BlockSpec(memory_space=pltpu.VMEM),
        scratch_shapes=[
            pltpu.SemaphoreType.DMA((NZ,)),
            pltpu.SemaphoreType.DMA((NZ, NX - 1)),
            pltpu.SemaphoreType.DMA((NX * NZ,)),
            pltpu.SemaphoreType.DMA,
        ],
        compiler_params=pltpu.CompilerParams(collective_id=0, has_side_effects=True, vmem_limit_bytes=VMEM_LIMIT),
        name="gather_weights",
    )(w)


def scatter_kernel(hb_ref, dqkv_ref, dy_ref, ob_ref, out_ref, xs, xr, acc, zs, zr, send_x, recv_x, send_z, recv_z):
    x, z = place()
    rows = out_ref.shape[0]
    wide = rows * NZ
    cols = 3 * DH
    greet(x, z)

    def tile(xx):
        span = pl.ds(pl.multiple_of(lax.rem(xx + NX, NX) * wide, wide), wide)
        dims = (((0,), (0,)), ((), ()))
        left = lax.dot_general(hb_ref[:, span], dqkv_ref[...], dims, preferred_element_type=jnp.float32)
        right = lax.dot_general(dy_ref[:, span], ob_ref[...], dims, preferred_element_type=jnp.float32)
        return jnp.concatenate([left, right], axis=1)

    sends = []
    for i, k in enumerate((2, 1, 3)):
        xs[i] = tile(x + k).astype(xs.dtype)
        copy = pltpu.make_async_remote_copy(
            src_ref=xs.at[i],
            dst_ref=xr.at[i],
            send_sem=send_x.at[i],
            recv_sem=recv_x.at[i],
            device_id={"dp": dp_of(x + k, z)},
            device_id_type=MESH,
        )
        copy.start()
        sends.append(copy)
    acc[...] = tile(x)
    for copy in sends:
        copy.wait_recv()
    acc[...] += (xr[0].astype(jnp.float32) + xr[1].astype(jnp.float32)) + xr[2].astype(jnp.float32)

    def mine(zz):
        return acc[pl.ds(pl.multiple_of(lax.rem(zz + 2 * NZ, NZ) * rows, rows), rows), :]

    half = NZ // 2
    hops = {}
    for step in range(half):
        for d, way, reach in ((0, 1, half - 1), (1, -1, half)):
            if step >= reach:
                continue
            part = mine(z + way * (reach - step))
            if step > 0:
                hops[d, step - 1].wait_recv()
                part = part + zr[d, step - 1].astype(jnp.float32)
            zs[d, step] = part.astype(zs.dtype)
            copy = pltpu.make_async_remote_copy(
                src_ref=zs.at[d, step],
                dst_ref=zr.at[d, step],
                send_sem=send_z.at[d, step],
                recv_sem=recv_z.at[d, step],
                device_id={"dp": dp_of(x, z + way)},
                device_id_type=MESH,
            )
            copy.start()
            hops[d, step] = copy
    hops[0, half - 2].wait_recv()
    hops[1, half - 1].wait_recv()
    out_ref[...] = mine(z) + (zr[0, half - 2].astype(jnp.float32) + zr[1, half - 1].astype(jnp.float32))
    for copy in sends:
        copy.wait_send()
    for copy in hops.values():
        copy.wait_send()


def scatter_grads(hb, dqkv, dy, ob):
    depth = hb.shape[1]
    rows = depth // (NX * NZ)
    wide = depth // NX
    half = NZ // 2
    return pl.pallas_call(
        scatter_kernel,
        out_shape=jax.ShapeDtypeStruct((rows, 4 * DH), jnp.float32),
        in_specs=[pl.BlockSpec(memory_space=pltpu.VMEM)] * 4,
        out_specs=pl.BlockSpec(memory_space=pltpu.VMEM),
        scratch_shapes=[
            pltpu.VMEM((NX - 1, wide, 4 * DH), jnp.bfloat16),
            pltpu.VMEM((NX - 1, wide, 4 * DH), jnp.bfloat16),
            pltpu.VMEM((wide, 4 * DH), jnp.float32),
            pltpu.VMEM((2, half, rows, 4 * DH), jnp.bfloat16),
            pltpu.VMEM((2, half, rows, 4 * DH), jnp.bfloat16),
            pltpu.SemaphoreType.DMA((NX - 1,)),
            pltpu.SemaphoreType.DMA((NX - 1,)),
            pltpu.SemaphoreType.DMA((2, half)),
            pltpu.SemaphoreType.DMA((2, half)),
        ],
        compiler_params=pltpu.CompilerParams(collective_id=1, has_side_effects=True, vmem_limit_bytes=VMEM_LIMIT),
        name="scatter_grads",
    )(hb, dqkv, dy, ob)


def for_sending(array):
    return jax.tree.map(lambda a: a.astype(jnp.bfloat16) if a.dtype == jnp.float32 else a, array)


def passed_along(block, axis, distance):
    devices = range(lax.axis_size(axis))
    route = [(i - distance, i) for i in devices if i - distance in devices]
    return lax.ppermute(block, axis, route)


def body(acts, cotangent, weights, doc_ids, lang_ids, temper):
    section_count = lax.axis_size("section")
    section_index = lax.axis_index("section")
    layer_in = acts[0]
    tok_count = layer_in.shape[0]
    head_size = DH
    full_weight = gather_weights(weights[0])
    w_qkv = full_weight[:, : 3 * head_size]
    w_out = full_weight[:, 3 * head_size :]
    inputs_wide = layer_in.astype(jnp.float32)
    inv_rms = lax.rsqrt(jnp.mean(inputs_wide * inputs_wide, axis=1, keepdims=True) + 1e-05)
    normed = (inputs_wide * inv_rms).astype(jnp.bfloat16)
    projected = jnp.dot(normed, w_qkv, preferred_element_type=jnp.float32).astype(jnp.bfloat16)
    query_rows = projected[:, :head_size]
    key_rows = projected[:, head_size : 2 * head_size]
    value_rows = projected[:, 2 * head_size :]
    score_scale = head_size ** (-0.5)
    slot_count = doc_ids.shape[0]
    doc_tok = jnp.repeat(doc_ids, tok_count // slot_count)
    positions = lax.iota(jnp.int32, tok_count)
    allowed = (doc_tok[:, None] == doc_tok[None, :]) & (positions[None, :] <= positions[:, None])
    scores = (
        jnp.einsum("qd,kd->qk", query_rows, key_rows, preferred_element_type=jnp.float32)
        * score_scale
    )
    exp_terms = jnp.where(allowed, jnp.exp(scores), jnp.float32(0.0))
    attn_probs = exp_terms / jnp.sum(exp_terms, axis=1, keepdims=True)
    probs_low = attn_probs.astype(jnp.bfloat16)
    attended = jnp.dot(probs_low, value_rows, preferred_element_type=jnp.float32)
    attended_low = attended.astype(jnp.bfloat16)
    doc_hot = doc_tok[:, None] == lax.iota(jnp.int32, slot_count)[None, :]
    lang_tok = jnp.sum(jnp.where(doc_hot, lang_ids[None, :], 0), axis=1)
    lang_hot = lang_tok[:, None] == lax.iota(jnp.int32, temper.shape[0])[None, :]
    tok_weight = jnp.sum(
        jnp.where(lang_hot, temper[None, :], jnp.float32(0.0)), axis=1, keepdims=True
    )
    top_grad = (cotangent.astype(jnp.float32) * tok_weight).astype(jnp.bfloat16)
    is_top = section_index == section_count - 1
    block_count = 2
    block_rows = tok_count // block_count

    def block_work(block_idx, state):
        incoming, key_acc, value_acc, grad_buf, proj_buf = state
        row_start = block_idx * block_rows
        row_stop = row_start + block_rows
        grad_in = jnp.where(is_top, top_grad[row_start:row_stop], incoming)
        out_grad = jnp.dot(grad_in, w_out, preferred_element_type=jnp.float32).astype(jnp.bfloat16)
        prob_grad = jnp.einsum(
            "qd,kd->qk", out_grad, value_rows, preferred_element_type=jnp.float32
        )
        row_delta = jnp.sum(
            out_grad.astype(jnp.float32) * attended[row_start:row_stop], axis=1, keepdims=True
        )
        score_grad = (
            attn_probs[row_start:row_stop, :tok_count] * (prob_grad - row_delta) * score_scale
        ).astype(jnp.bfloat16)
        query_grad = jnp.dot(score_grad, key_rows, preferred_element_type=jnp.float32).astype(
            jnp.bfloat16
        )
        key_acc = key_acc.at[:tok_count].add(
            jnp.einsum(
                "qk,qd->kd",
                score_grad,
                query_rows[row_start:row_stop],
                preferred_element_type=jnp.float32,
            )
        )
        value_acc = value_acc.at[:tok_count].add(
            jnp.einsum(
                "qk,qd->kd",
                probs_low[row_start:row_stop, :tok_count],
                out_grad,
                preferred_element_type=jnp.float32,
            )
        )
        proj_grad = jnp.concatenate(
            [
                query_grad,
                key_acc[row_start:row_stop].astype(jnp.bfloat16),
                value_acc[row_start:row_stop].astype(jnp.bfloat16),
            ],
            axis=1,
        )
        normed_grad = jnp.einsum("qe,de->qd", proj_grad, w_qkv, preferred_element_type=jnp.float32)
        block_in = layer_in[row_start:row_stop].astype(jnp.float32)
        block_inv = inv_rms[row_start:row_stop]
        inv_cube = block_inv * block_inv * block_inv
        input_grad = (
            grad_in.astype(jnp.float32)
            + block_inv * normed_grad
            - block_in * inv_cube * jnp.mean(normed_grad * block_in, axis=1, keepdims=True)
        )
        grad_buf = grad_buf.at[row_start:row_stop].set(grad_in)
        proj_buf = proj_buf.at[row_start:row_stop].set(proj_grad)
        return (input_grad.astype(jnp.bfloat16), key_acc, value_acc, grad_buf, proj_buf)

    def spare_block(state):
        incoming, key_acc, value_acc, grad_buf, proj_buf = state
        return (jnp.zeros_like(incoming), key_acc, value_acc, grad_buf, proj_buf)

    branches = [partial(block_work, block_idx) for block_idx in range(block_count)] + [spare_block]

    def chain_step(step_idx, carried):
        block_idx = block_count - 1 - step_idx + (section_count - 1 - section_index)
        active = (block_idx >= 0) & (block_idx < block_count)
        branch_idx = jnp.where(active, block_idx, block_count)
        sent_block, key_acc, value_acc, grad_buf, proj_buf = lax.switch(
            branch_idx, branches, carried
        )
        received = jax.tree.map(
            lambda part, own: part.astype(own.dtype),
            passed_along(for_sending(sent_block), "section", -1),
            sent_block,
        )
        return (received, key_acc, value_acc, grad_buf, proj_buf)

    start_state = (
        jnp.zeros((block_rows, layer_in.shape[1]), jnp.bfloat16),
        jnp.zeros((tok_count, head_size), jnp.float32),
        jnp.zeros((tok_count, head_size), jnp.float32),
        jnp.zeros((tok_count, layer_in.shape[1]), jnp.bfloat16),
        jnp.zeros((tok_count, 3 * head_size), jnp.bfloat16),
    )
    end_state = lax.fori_loop(0, section_count + block_count - 1, chain_step, start_state)
    grad_buf = end_state[3]
    proj_buf = end_state[4]
    summed = scatter_grads(normed, proj_buf, grad_buf, attended_low)
    return summed[None]


def solution(mesh):
    return jax.shard_map(
        body,
        mesh=mesh,
        in_specs=(
            P("section", "dp", None),
            P("dp", None),
            P("section", "dp", None),
            P("dp"),
            P("dp"),
            P(),
        ),
        out_specs=P("section", "dp", None),
        check_vma=False,
    )
```

```python
from functools import partial

import jax
import jax.numpy as jnp
from jax import lax
from jax.experimental import pallas as pl
from jax.experimental.pallas import tpu as pltpu
from jax.sharding import PartitionSpec as P

DH = 64
WIDE = 4 * DH
MESH = pl.DeviceIdType.MESH
NX = 4
NZ = 16
ROWS = 32
FIRST = 16
VMEM_LIMIT = 58 << 20
F32 = jnp.float32
BF16 = jnp.bfloat16
NT = (((1,), (1,)), ((), ()))
TN = (((0,), (0,)), ((), ()))


def mm(a, b, dims=(((1,), (0,)), ((), ()))):
    return lax.dot_general(a, b, dims, preferred_element_type=F32)


def dp_of(x, z):
    return lax.rem(x + NX, NX) * NZ + lax.rem(z + 2 * NZ, NZ)


def remote(src, dst, send, recv, device):
    return pltpu.make_async_remote_copy(
        src_ref=src, dst_ref=dst, send_sem=send, recv_sem=recv, device_id=device, device_id_type=MESH
    )


def arrived(dst, sem):
    pltpu.make_async_copy(dst, dst, sem).wait()


def body_kernel(
    sections, doc_ref, lang_ref, temper_ref, acts_hbm, cot_hbm, w_ref, out_ref,
    x_ref, cot_ref, wf, hb, dy, dx, inv_ref, qkvf, qkvb, kpad, qpad, prob, probb, att, attb, acc, dqkv,
    xs, xr, tot, zs, zr,
    load_sem, own_sem, ga_xs, ga_xr, ga_zs, ga_zr, gb_zs, gb_zr, gb_xs, gb_xr, ch_s, ch_r, sc_xs, sc_xr, sc_zs, sc_zr,
):
    s = lax.axis_index("section")
    me = lax.axis_index("dp")
    x, z = me // NZ, lax.rem(me, NZ)
    toks, depth = x_ref.shape
    part = w_ref.shape[0]
    half = NZ // 2
    blocks = toks // ROWS
    wide = depth // NX

    loads = [
        pltpu.make_async_copy(acts_hbm.at[0], x_ref, load_sem.at[0]),
        pltpu.make_async_copy(cot_hbm, cot_ref, load_sem.at[1]),
        pltpu.make_async_copy(w_ref, wf.at[x, z], own_sem),
    ]
    for copy in loads:
        copy.start()
    barrier = pltpu.get_barrier_semaphore()
    others = [{"dp": dp_of(x, z + 1)}, {"dp": dp_of(x, z - 1)}]
    others += [{"dp": dp_of(x + k, z)} for k in range(1, NX)]
    others += [{"section": lax.rem(s + 1, sections)}, {"section": lax.rem(s + sections - 1, sections)}]
    for other in others:
        pl.semaphore_signal(barrier, inc=1, device_id=other, device_id_type=MESH)
    pl.semaphore_wait(barrier, len(others))

    sends = []

    def go(copy):
        copy.start()
        sends.append(copy)

    first, rest = pl.ds(0, FIRST), pl.ds(FIRST, part - FIRST)
    for k in range(1, NX):
        go(remote(w_ref.at[first], wf.at[x, z, first], ga_xs.at[k - 1], ga_xr.at[k - 1], {"dp": dp_of(x + k, z)}))
    for d, way in ((0, 1), (1, -1)):
        go(remote(w_ref.at[rest], wf.at[x, z, rest], gb_zs.at[d, 0], gb_zr.at[d, 0], {"dp": dp_of(x, z + way)}))
    for k in range(1, NX):
        go(remote(w_ref.at[rest], wf.at[x, z, rest], gb_xs.at[k - 1, 0], gb_xr.at[k - 1, 0], {"dp": dp_of(x + k, z)}))

    def normalise(i, carry):
        rows = pl.ds(pl.multiple_of(i * ROWS, ROWS), ROWS)
        wide_x = x_ref[rows, :].astype(F32)
        inv = lax.rsqrt(jnp.sum(wide_x * wide_x, axis=1, keepdims=True) / depth + 1e-05)
        inv_ref[rows, :] = inv
        hb[rows, :] = (wide_x * inv).astype(BF16)
        return carry

    loads[0].wait()
    lax.fori_loop(0, blocks, normalise, 0)
    loads[1].wait()
    loads[2].wait()

    for k in range(1, NX):
        arrived(wf.at[lax.rem(x + NX - k, NX), z, first], ga_xr.at[k - 1])
    slot = 0
    for step in range(half + 1):
        for d, way, reach in ((0, 1, half), (1, -1, half - 1)):
            if step > reach:
                continue
            zz = lax.rem(z - way * step + 2 * NZ, NZ)
            if step > 0:
                arrived(wf.at[x, zz, rest], gb_zr.at[d, step - 1])
                if step < reach:
                    go(remote(wf.at[x, zz, rest], wf.at[x, zz, rest], gb_zs.at[d, step], gb_zr.at[d, step], {"dp": dp_of(x, z + way)}))
                slot += 1
                for k in range(1, NX):
                    go(remote(wf.at[x, zz, rest], wf.at[x, zz, rest], gb_xs.at[k - 1, slot], gb_xr.at[k - 1, slot], {"dp": dp_of(x + k, z)}))
                arrived(wf.at[:, zz, first], ga_zr.at[d, step - 1])
            if step < reach:
                go(remote(wf.at[:, zz, first], wf.at[:, zz, first], ga_zs.at[d, step], ga_zr.at[d, step], {"dp": dp_of(x, z + way)}))

    @pl.when(s == sections - 1)
    def _():
        weights = [temper_ref[lang_ref[doc_ref[i]]] for i in range(2)]

        def temper_rows(i, carry):
            rows = pl.ds(pl.multiple_of(i * ROWS, ROWS), ROWS)
            index = i * ROWS + lax.broadcasted_iota(jnp.int32, (ROWS, 1), 0)
            level = jnp.where(index < toks // 2, weights[0], weights[1])
            dy[rows, :] = (cot_ref[rows, :].astype(F32) * level).astype(BF16)
            return carry

        lax.fori_loop(0, blocks, temper_rows, 0)

    slot = 0
    for k in range(1, NX):
        arrived(wf.at[lax.rem(x + NX - k, NX), z, rest], gb_xr.at[k - 1, 0])
    for step in range(1, half + 1):
        for d, way, reach in ((0, 1, half), (1, -1, half - 1)):
            if step > reach:
                continue
            zz = lax.rem(z - way * step + 2 * NZ, NZ)
            slot += 1
            for k in range(1, NX):
                arrived(wf.at[lax.rem(x + NX - k, NX), zz, rest], gb_xr.at[k - 1, slot])

    def project(left, rows):
        total = None
        for xx in range(NX):
            term = mm(left[rows, pl.ds(xx * wide, wide)], wf[xx].reshape(wide, WIDE))
            total = term if total is None else total + term
        return total

    lane = lax.broadcasted_iota(jnp.int32, (1, WIDE), 1)
    is_q, is_k = lane < DH, (lane >= DH) & (lane < 2 * DH)
    is_v = (lane >= 2 * DH) & (lane < 3 * DH)
    scale = DH ** (-0.5)

    everything = pl.ds(0, toks)
    qkv = project(hb, everything)
    qkvf[...] = qkv
    low = qkv.astype(BF16)
    qkvb[...] = low
    keys = jnp.where(is_q, pltpu.roll(qkv, WIDE - DH, 1), 0.0).astype(BF16)
    kpad[...] = keys
    qpad[...] = jnp.where(is_k, pltpu.roll(qkv, DH, 1), 0.0).astype(BF16)
    queries = jnp.where(is_q, qkv, 0.0).astype(BF16)
    row = lax.broadcasted_iota(jnp.int32, (toks, toks), 0)
    col = lax.broadcasted_iota(jnp.int32, (toks, toks), 1)
    joined = (jnp.full((toks, toks), doc_ref[0], jnp.int32) == jnp.full((toks, toks), doc_ref[1], jnp.int32))
    allowed = (col <= row) & (joined | ((row < toks // 2) == (col < toks // 2)))
    terms = jnp.where(allowed, jnp.exp(mm(queries, keys, NT) * scale), 0.0)
    probs = terms / jnp.sum(terms, axis=1, keepdims=True)
    prob[...] = probs
    probb[...] = probs.astype(BF16)
    attended = jnp.where(is_v, mm(probs.astype(BF16), low), 0.0)
    att[...] = attended
    attb[...] = pltpu.roll(attended, DH, 1).astype(BF16)
    acc[...] = jnp.zeros_like(acc)

    def chain(i, carry):
        block = blocks - 1 - i
        rows = pl.ds(pl.multiple_of(block * ROWS, ROWS), ROWS)

        @pl.when(s < sections - 1)
        def _():
            arrived(dy.at[rows], ch_r.at[block])

        out_grad = jnp.where(is_v, pltpu.roll(project(dy, rows), WIDE - DH, 1), 0.0).astype(BF16)
        delta = jnp.sum(out_grad.astype(F32) * att[rows, :], axis=1, keepdims=True)
        prob_grad = mm(out_grad, qkvb[...], NT)
        score_grad = (prob[rows, :] * (prob_grad - delta) * scale).astype(BF16)
        acc[...] += mm(score_grad, qpad[rows, :], TN) + mm(probb[rows, :], out_grad, TN)
        proj_grad = (mm(score_grad, kpad[...]) + acc[rows, :]).astype(BF16)
        dqkv[rows, :] = proj_grad

        @pl.when(s > 0)
        def _():
            inv = inv_ref[rows, :]
            pull = inv * inv * (jnp.sum(proj_grad.astype(F32) * qkvf[rows, :], axis=1, keepdims=True) / depth)
            for xx in range(NX):
                span = pl.ds(xx * wide, wide)
                back = mm(proj_grad, wf[xx].reshape(wide, WIDE), NT)
                dx[rows, span] = (
                    dy[rows, span].astype(F32) + inv * back - x_ref[rows, span].astype(F32) * pull
                ).astype(BF16)
            remote(dx.at[rows], dy.at[rows], ch_s.at[block], ch_r.at[block], {"section": s - 1}).start()

        return carry

    lax.fori_loop(0, blocks, chain, 0)

    def tile(xx):
        span = pl.ds(pl.multiple_of(lax.rem(xx + NX, NX) * wide, wide), wide)
        return mm(hb[:, span], dqkv[...], TN) + mm(dy[:, span], attb[...], TN)

    hops = {}
    for i, k in enumerate([2, 1, 3][-(NX - 1):] if NX == 4 else range(1, NX)):
        xs[i] = tile(x + k).astype(BF16)
        hops["x", i] = remote(xs.at[i], xr.at[i], sc_xs.at[i], sc_xr.at[i], {"dp": dp_of(x + k, z)})
        go(hops["x", i])
    tot[...] = tile(x)
    for i in range(NX - 1):
        hops["x", i].wait_recv()
        tot[...] += xr[i].astype(F32)

    def mine(zz):
        return tot[pl.ds(pl.multiple_of(lax.rem(zz + 2 * NZ, NZ) * part, part), part), :]

    for step in range(half):
        for d, way, reach in ((0, 1, half - 1), (1, -1, half)):
            if step >= reach:
                continue
            partial_sum = mine(z + way * (reach - step))
            if step > 0:
                hops[d, step - 1].wait_recv()
                partial_sum = partial_sum + zr[d, step - 1].astype(F32)
            zs[d, step] = partial_sum.astype(BF16)
            hops[d, step] = remote(zs.at[d, step], zr.at[d, step], sc_zs.at[d, step], sc_zr.at[d, step], {"dp": dp_of(x, z + way)})
            go(hops[d, step])
    hops[0, half - 2].wait_recv()
    hops[1, half - 1].wait_recv()
    out_ref[...] = mine(z) + (zr[0, half - 2].astype(F32) + zr[1, half - 1].astype(F32))
    for copy in sends:
        copy.wait_send()

    @pl.when(s > 0)
    def _():
        def drain(i, carry):
            rows = pl.ds(pl.multiple_of(i * ROWS, ROWS), ROWS)
            remote(dx.at[rows], dy.at[rows], ch_s.at[i], ch_r.at[i], {"section": s - 1}).wait_send()
            return carry

        lax.fori_loop(0, blocks, drain, 0)


def body(acts, cotangent, weights, doc_ids, lang_ids, temper):
    sections = lax.axis_size("section")
    toks, depth = cotangent.shape
    part = weights.shape[1]
    half = NZ // 2
    wide = depth // NX
    blocks = toks // ROWS
    dma = pltpu.SemaphoreType.DMA
    vmem = pltpu.VMEM
    smem = pl.BlockSpec(memory_space=pltpu.SMEM)
    hbm = pl.BlockSpec(memory_space=pl.ANY)
    grads = pl.pallas_call(
        partial(body_kernel, sections),
        out_shape=jax.ShapeDtypeStruct((part, WIDE), F32),
        in_specs=[smem, smem, smem, hbm, hbm, pl.BlockSpec(memory_space=pltpu.VMEM)],
        out_specs=pl.BlockSpec(memory_space=pltpu.VMEM),
        scratch_shapes=[
            vmem((toks, depth), BF16),
            vmem((toks, depth), BF16),
            vmem((NX, NZ, part, WIDE), BF16),
            vmem((toks, depth), BF16),
            vmem((toks, depth), BF16),
            vmem((toks, depth), BF16),
            vmem((toks, 1), F32),
            vmem((toks, WIDE), F32),
            vmem((toks, WIDE), BF16),
            vmem((toks, WIDE), BF16),
            vmem((toks, WIDE), BF16),
            vmem((toks, toks), F32),
            vmem((toks, toks), BF16),
            vmem((toks, WIDE), F32),
            vmem((toks, WIDE), BF16),
            vmem((toks, WIDE), F32),
            vmem((toks, WIDE), BF16),
            vmem((NX - 1, wide, WIDE), BF16),
            vmem((NX - 1, wide, WIDE), BF16),
            vmem((wide, WIDE), F32),
            vmem((2, half, part, WIDE), BF16),
            vmem((2, half, part, WIDE), BF16),
            dma((2,)),
            dma,
            dma((NX - 1,)),
            dma((NX - 1,)),
            dma((2, half)),
            dma((2, half)),
            dma((2, half)),
            dma((2, half)),
            dma((NX - 1, NZ)),
            dma((NX - 1, NZ)),
            dma((blocks,)),
            dma((blocks,)),
            dma((NX - 1,)),
            dma((NX - 1,)),
            dma((2, half)),
            dma((2, half)),
        ],
        compiler_params=pltpu.CompilerParams(collective_id=0, has_side_effects=True, vmem_limit_bytes=VMEM_LIMIT),
        name="layer_chain",
    )(doc_ids, lang_ids, temper, acts, cotangent, weights[0])
    return grads[None]


def solution(mesh):
    return jax.shard_map(
        body,
        mesh=mesh,
        in_specs=(
            P("section", "dp", None),
            P("dp", None),
            P("section", "dp", None),
            P("dp"),
            P("dp"),
            P(),
        ),
        out_specs=P("section", "dp", None),
        check_vma=False,
    )
```

```python
from functools import partial

import jax
import jax.numpy as jnp
from jax import lax
from jax.experimental import pallas as pl
from jax.experimental.pallas import tpu as pltpu
from jax.sharding import PartitionSpec as P

DH = 64
WIDE = 4 * DH
MESH = pl.DeviceIdType.MESH
NX = 4
NZ = 16
ROWS = 32
FAR = (8, 4, -4)
NEAR = ((2, 0, 2), (-2, 2, 2), (1, 0, 4), (-1, 0, 4))
TURN = (2, 1, 3)
LATE = 2
SPLIT = 2
VMEM_LIMIT = 58 << 20
F32 = jnp.float32
BF16 = jnp.bfloat16
NT = (((1,), (1,)), ((), ()))
TN = (((0,), (0,)), ((), ()))


def mm(a, b, dims=(((1,), (0,)), ((), ()))):
    return lax.dot_general(a, b, dims, preferred_element_type=F32)


def x_of(x):
    return lax.rem(x + 2 * NX, NX)


def z_of(z):
    return lax.rem(z + 2 * NZ, NZ)


def dp_of(x, z):
    return x_of(x) * NZ + z_of(z)


def remote(src, dst, send, recv, device):
    return pltpu.make_async_remote_copy(
        src_ref=src, dst_ref=dst, send_sem=send, recv_sem=recv, device_id=device, device_id_type=MESH
    )


def arrived(dst, sem):
    pltpu.make_async_copy(dst, dst, sem).wait()


def body_kernel(
    sections, doc_ref, lang_ref, temper_ref, acts_hbm, cot_hbm, w_ref, out_ref,
    x_ref, cot_ref, wf, hb, dy, dx, inv_ref, qkvf, qkvb, kpad, qpad, prob, probb, att, attb, acc, dqkv,
    hbx, obx, dyx, dqx, xs, xr, tot, near_s, near_r, far_s, far_r,
    load_sem, own_sem, gz_s, gz_r, gx_s, gx_r, ch_s, ch_r, hx_s, hx_r, ox_s, ox_r, yx_s, yx_r, qx_s, qx_r, sx_s, sx_r,
    sn_s, sn_r, sf_s, sf_r,
):
    s = lax.axis_index("section")
    me = lax.axis_index("dp")
    x, z = me // NZ, lax.rem(me, NZ)
    toks, depth = x_ref.shape
    part = w_ref.shape[0]
    blocks = toks // ROWS
    wide = depth // NX

    loads = [
        pltpu.make_async_copy(acts_hbm.at[0], x_ref, load_sem.at[0]),
        pltpu.make_async_copy(cot_hbm, cot_ref, load_sem.at[1]),
        pltpu.make_async_copy(w_ref, wf.at[x, z], own_sem),
    ]
    for copy in loads:
        copy.start()
    barrier = pltpu.get_barrier_semaphore()
    reach = FAR + tuple(d for d, start, size in NEAR)
    others = [{"dp": dp_of(x, z + d)} for d in sorted({d % NZ for d in reach} | {-d % NZ for d in reach})]
    others += [{"dp": dp_of(x + k, z)} for k in range(1, NX)]
    others += [{"section": lax.rem(s + 1, sections)}, {"section": lax.rem(s + sections - 1, sections)}]
    for other in others:
        pl.semaphore_signal(barrier, inc=1, device_id=other, device_id_type=MESH)
    pl.semaphore_wait(barrier, len(others))

    sends = []

    def go(copy):
        copy.start()
        sends.append(copy)

    late = []
    quarter = part // 4
    everyone = pl.ds(0, part)
    near_rows = [pl.ds(start * quarter, size * quarter) for d, start, size in NEAR]

    def put(src, ahead, rows, index, d):
        dst = wf.at[x, z_of(z + ahead), rows]
        src = dst if src is None else src.at[rows]
        go(remote(src, dst, gz_s.at[index], gz_r.at[index], {"dp": dp_of(x, z + d)}))
        return (ahead - d, rows, gz_r.at[index])

    def across(src, ahead, rows, index):
        dst = wf.at[x, z_of(z + ahead), rows]
        src = dst if src is None else src.at[rows]
        for k in TURN:
            go(remote(src, dst, gx_s.at[k - 1, index], gx_r.at[k - 1, index], {"dp": dp_of(x + k, z)}))
            late.append((k, ahead, rows, index))

    n_far, n_near = len(FAR), len(NEAR)
    far_in = [put(w_ref, 0, everyone, i, d) for i, d in enumerate(FAR)]
    near_in = [put(w_ref, 0, near_rows[i], n_far + i, d) for i, (d, start, size) in enumerate(NEAR)]
    across(w_ref, 0, everyone, 0)

    def normalise(i, carry):
        rows = pl.ds(pl.multiple_of(i * ROWS, ROWS), ROWS)
        wide_x = x_ref[rows, :].astype(F32)
        inv = lax.rsqrt(jnp.sum(wide_x * wide_x, axis=1, keepdims=True) / depth + 1e-05)
        inv_ref[rows, :] = inv
        hb[rows, :] = (wide_x * inv).astype(BF16)
        return carry

    loads[0].wait()
    lax.fori_loop(0, blocks, normalise, 0)
    loads[1].wait()
    loads[2].wait()

    for j, (ahead, rows, recv) in enumerate(far_in):
        arrived(wf.at[x, z_of(z + ahead), rows], recv)
        for i, (d, start, size) in enumerate(NEAR):
            near_in.append(put(None, ahead, near_rows[i], n_far + (j + 1) * n_near + i, d))
    for j, (ahead, rows, recv) in enumerate(far_in):
        across(None, ahead, rows, 1 + j)
    for j, (ahead, rows, recv) in enumerate(near_in):
        arrived(wf.at[x, z_of(z + ahead), rows], recv)
        across(None, ahead, rows, 1 + n_far + j)

    @pl.when(s == sections - 1)
    def _():
        weights = [temper_ref[lang_ref[doc_ref[i]]] for i in range(2)]

        def temper_rows(i, carry):
            rows = pl.ds(pl.multiple_of(i * ROWS, ROWS), ROWS)
            index = i * ROWS + lax.broadcasted_iota(jnp.int32, (ROWS, 1), 0)
            level = jnp.where(index < toks // 2, weights[0], weights[1])
            dy[rows, :] = (cot_ref[rows, :].astype(F32) * level).astype(BF16)
            return carry

        lax.fori_loop(0, blocks, temper_rows, 0)

    for k, ahead, rows, index in late:
        arrived(wf.at[x_of(x - k), z_of(z + ahead), rows], gx_r.at[k - 1, index])

    def columns(k):
        return pl.ds(pl.multiple_of(x_of(x + k) * wide, wide), wide)

    peers = [(k - 1, k, {"dp": dp_of(x + k, z)}) for k in TURN]
    share_hb = [remote(hb.at[:, columns(k)], hbx.at[j], hx_s.at[j], hx_r.at[j], device) for j, k, device in peers]

    @pl.when(s < sections - LATE)
    def _():
        for copy in share_hb:
            copy.start()

    def project(left, rows):
        total = None
        for xx in range(NX):
            term = mm(left[rows, pl.ds(xx * wide, wide)], wf[xx].reshape(wide, WIDE))
            total = term if total is None else total + term
        return total

    lane = lax.broadcasted_iota(jnp.int32, (1, WIDE), 1)
    is_q, is_k = lane < DH, (lane >= DH) & (lane < 2 * DH)
    is_v = (lane >= 2 * DH) & (lane < 3 * DH)
    scale = DH ** (-0.5)

    everything = pl.ds(0, toks)
    qkv = project(hb, everything)
    qkvf[...] = qkv
    low = qkv.astype(BF16)
    qkvb[...] = low
    keys = jnp.where(is_q, pltpu.roll(qkv, WIDE - DH, 1), 0.0).astype(BF16)
    kpad[...] = keys
    qpad[...] = jnp.where(is_k, pltpu.roll(qkv, DH, 1), 0.0).astype(BF16)
    queries = jnp.where(is_q, qkv, 0.0).astype(BF16)
    row = lax.broadcasted_iota(jnp.int32, (toks, toks), 0)
    col = lax.broadcasted_iota(jnp.int32, (toks, toks), 1)
    joined = (jnp.full((toks, toks), doc_ref[0], jnp.int32) == jnp.full((toks, toks), doc_ref[1], jnp.int32))
    allowed = (col <= row) & (joined | ((row < toks // 2) == (col < toks // 2)))
    terms = jnp.where(allowed, jnp.exp(mm(queries, keys, NT) * scale), 0.0)
    probs = terms / jnp.sum(terms, axis=1, keepdims=True)
    prob[...] = probs
    probb[...] = probs.astype(BF16)
    attended = jnp.where(is_v, mm(probs.astype(BF16), low), 0.0)
    att[...] = attended
    attb[...] = pltpu.roll(attended, DH, 1).astype(BF16)
    acc[...] = jnp.zeros_like(acc)
    share_ob = [remote(attb, obx.at[j], ox_s.at[j], ox_r.at[j], device) for j, k, device in peers]

    @pl.when(s < sections - LATE)
    def _():
        for copy in share_ob:
            copy.start()

    def share_dy(block):
        rows = pl.ds(pl.multiple_of(block * ROWS, ROWS), ROWS)
        return [
            remote(dy.at[rows, columns(k)], dyx.at[j, rows], yx_s.at[j, block], yx_r.at[j, block], device)
            for j, k, device in peers
        ]

    def share_dq(block):
        rows = pl.ds(pl.multiple_of(block * ROWS, ROWS), ROWS)
        return [
            remote(dqkv.at[rows], dqx.at[j, rows], qx_s.at[j, block], qx_r.at[j, block], device)
            for j, k, device in peers
        ]

    group = NX // SPLIT

    def pass_down(block, i):
        at = (pl.ds(pl.multiple_of(block * ROWS, ROWS), ROWS), pl.ds(i * group * wide, group * wide))
        return remote(dx.at[at], dy.at[at], ch_s.at[i, block], ch_r.at[i, block], {"section": s - 1})

    def chain(i, carry):
        block = blocks - 1 - i
        rows = pl.ds(pl.multiple_of(block * ROWS, ROWS), ROWS)

        projected = None
        for xx in range(NX):

            if xx % group == 0:

                @pl.when(s < sections - 1)
                def _():
                    arrived(dy.at[rows, pl.ds(xx * wide, group * wide)], ch_r.at[xx // group, block])

            term = mm(dy[rows, pl.ds(xx * wide, wide)], wf[xx].reshape(wide, WIDE))
            projected = term if projected is None else projected + term

        @pl.when(s == 0)
        def _():
            for copy in share_dy(block):
                copy.start()

        out_grad = jnp.where(is_v, pltpu.roll(projected, WIDE - DH, 1), 0.0).astype(BF16)
        delta = jnp.sum(out_grad.astype(F32) * att[rows, :], axis=1, keepdims=True)
        prob_grad = mm(out_grad, qkvb[...], NT)
        score_grad = (prob[rows, :] * (prob_grad - delta) * scale).astype(BF16)
        acc[...] += mm(score_grad, qpad[rows, :], TN) + mm(probb[rows, :], out_grad, TN)
        proj_grad = (mm(score_grad, kpad[...]) + acc[rows, :]).astype(BF16)
        dqkv[rows, :] = proj_grad

        @pl.when(s > 0)
        def _():
            inv = inv_ref[rows, :]
            pull = inv * inv * (jnp.sum(proj_grad.astype(F32) * qkvf[rows, :], axis=1, keepdims=True) / depth)
            for xx in range(NX):
                span = pl.ds(xx * wide, wide)
                back = mm(proj_grad, wf[xx].reshape(wide, WIDE), NT)
                dx[rows, span] = (
                    dy[rows, span].astype(F32) + inv * back - x_ref[rows, span].astype(F32) * pull
                ).astype(BF16)
                if (xx + 1) % group == 0:
                    pass_down(block, xx // group).start()

        @pl.when((s > 0) & (s < sections - LATE))
        def _():
            for copy in share_dy(block):
                copy.start()

        @pl.when(s < sections - LATE)
        def _():
            for copy in share_dq(block):
                copy.start()

        return carry

    lax.fori_loop(0, blocks, chain, 0)

    def tile(k):
        return mm(hb[:, columns(k)], dqkv[...], TN) + mm(dy[:, columns(k)], attb[...], TN)

    @pl.when(s >= sections - LATE)
    def _():
        swaps = []
        for j, k, device in peers:
            xs[j] = tile(k).astype(BF16)
            swaps.append(remote(xs.at[j], xr.at[j], sx_s.at[j], sx_r.at[j], device))
            swaps[-1].start()
        tot[...] = tile(0)
        for i, (j, k, device) in enumerate(peers):
            swaps[i].wait()
            tot[...] += xr[j].astype(F32)

    @pl.when(s < sections - LATE)
    def _():
        tot[...] = tile(0)
        for copy in share_hb + share_ob:
            copy.wait()

        def landed(i, carry):
            for copy in share_dy(i) + share_dq(i):
                copy.wait()
            return carry

        lax.fori_loop(0, blocks, landed, 0)
        for j, k, device in peers:
            tot[...] += mm(hbx[j], dqx[j], TN) + mm(dyx[j], obx[j], TN)

    def mine(zz, start=0, size=4):
        first = z_of(zz) * part + start * quarter
        return tot[pl.ds(pl.multiple_of(first, quarter), size * quarter), :]

    ends = (0,) + FAR
    hops = []
    for i, (d, start, size) in enumerate(NEAR):
        rows = pl.ds(0, size * quarter)
        for j, a in enumerate(ends):
            near_s[i, j, rows, :] = mine(z + d + a, start, size).astype(BF16)
        hops.append(
            remote(near_s.at[i, :, rows], near_r.at[i, :, rows], sn_s.at[i], sn_r.at[i], {"dp": dp_of(x, z + d)})
        )
        go(hops[i])
    for copy in hops:
        copy.wait_recv()

    def gathered(j):
        halves = []
        for h in (0, 2):
            total = mine(z + ends[j], h, 2)
            for i, (d, start, size) in enumerate(NEAR):
                if start <= h < start + size:
                    total = total + near_r[i, j, pl.ds((h - start) * quarter, 2 * quarter), :].astype(F32)
            halves.append(total)
        return jnp.concatenate(halves, axis=0)

    hops = []
    for j, a in enumerate(FAR):
        far_s[j] = gathered(j + 1).astype(BF16)
        hops.append(remote(far_s.at[j], far_r.at[j], sf_s.at[j], sf_r.at[j], {"dp": dp_of(x, z + a)}))
        go(hops[j])
    total = gathered(0)
    for j, copy in enumerate(hops):
        copy.wait_recv()
        total = total + far_r[j].astype(F32)
    out_ref[...] = total
    for copy in sends:
        copy.wait_send()

    @pl.when(s > 0)
    def _():
        def drain(i, carry):
            for part_index in range(SPLIT):
                pass_down(i, part_index).wait_send()
            return carry

        lax.fori_loop(0, blocks, drain, 0)


def body(acts, cotangent, weights, doc_ids, lang_ids, temper):
    sections = lax.axis_size("section")
    toks, depth = cotangent.shape
    part = weights.shape[1]
    near, far = len(NEAR), len(FAR)
    slots = 1 + far + (1 + far) * near
    wide = depth // NX
    blocks = toks // ROWS
    dma = pltpu.SemaphoreType.DMA
    vmem = pltpu.VMEM
    smem = pl.BlockSpec(memory_space=pltpu.SMEM)
    hbm = pl.BlockSpec(memory_space=pl.ANY)
    grads = pl.pallas_call(
        partial(body_kernel, sections),
        out_shape=jax.ShapeDtypeStruct((part, WIDE), F32),
        in_specs=[smem, smem, smem, hbm, hbm, pl.BlockSpec(memory_space=pltpu.VMEM)],
        out_specs=pl.BlockSpec(memory_space=pltpu.VMEM),
        scratch_shapes=[
            vmem((toks, depth), BF16),
            vmem((toks, depth), BF16),
            vmem((NX, NZ, part, WIDE), BF16),
            vmem((toks, depth), BF16),
            vmem((toks, depth), BF16),
            vmem((toks, depth), BF16),
            vmem((toks, 1), F32),
            vmem((toks, WIDE), F32),
            vmem((toks, WIDE), BF16),
            vmem((toks, WIDE), BF16),
            vmem((toks, WIDE), BF16),
            vmem((toks, toks), F32),
            vmem((toks, toks), BF16),
            vmem((toks, WIDE), F32),
            vmem((toks, WIDE), BF16),
            vmem((toks, WIDE), F32),
            vmem((toks, WIDE), BF16),
            vmem((NX - 1, toks, wide), BF16),
            vmem((NX - 1, toks, WIDE), BF16),
            vmem((NX - 1, toks, wide), BF16),
            vmem((NX - 1, toks, WIDE), BF16),
            vmem((NX - 1, wide, WIDE), BF16),
            vmem((NX - 1, wide, WIDE), BF16),
            vmem((wide, WIDE), F32),
            vmem((near, far + 1, part, WIDE), BF16),
            vmem((near, far + 1, part, WIDE), BF16),
            vmem((far, part, WIDE), BF16),
            vmem((far, part, WIDE), BF16),
            dma((2,)),
            dma,
            dma((slots,)),
            dma((slots,)),
            dma((NX - 1, slots)),
            dma((NX - 1, slots)),
            dma((SPLIT, blocks)),
            dma((SPLIT, blocks)),
            dma((NX - 1,)),
            dma((NX - 1,)),
            dma((NX - 1,)),
            dma((NX - 1,)),
            dma((NX - 1, blocks)),
            dma((NX - 1, blocks)),
            dma((NX - 1, blocks)),
            dma((NX - 1, blocks)),
            dma((NX - 1,)),
            dma((NX - 1,)),
            dma((near,)),
            dma((near,)),
            dma((far,)),
            dma((far,)),
        ],
        compiler_params=pltpu.CompilerParams(collective_id=0, has_side_effects=True, vmem_limit_bytes=VMEM_LIMIT),
        name="layer_chain",
    )(doc_ids, lang_ids, temper, acts, cotangent, weights[0])
    return grads[None]


def solution(mesh):
    return jax.shard_map(
        body,
        mesh=mesh,
        in_specs=(
            P("section", "dp", None),
            P("dp", None),
            P("section", "dp", None),
            P("dp"),
            P("dp"),
            P(),
        ),
        out_specs=P("section", "dp", None),
        check_vma=False,
    )
```

```python
from functools import partial

import jax
import jax.numpy as jnp
from jax import lax
from jax.experimental import pallas as pl
from jax.experimental.pallas import tpu as pltpu
from jax.sharding import PartitionSpec as P

DH = 64
WIDE = 4 * DH
MESH = pl.DeviceIdType.MESH
NX = 4
NZ = 16
ROWS = 32
FAR = (8, 4, -4)
NEAR = ((2, 0, 2), (-2, 2, 2), (1, 0, 4), (-1, 0, 4))
TURN = (2, 1, 3)
LATE = 2
SPLIT = 4
VMEM_LIMIT = 58 << 20
F32 = jnp.float32
BF16 = jnp.bfloat16
NT = (((1,), (1,)), ((), ()))
TN = (((0,), (0,)), ((), ()))


def mm(a, b, dims=(((1,), (0,)), ((), ()))):
    return lax.dot_general(a, b, dims, preferred_element_type=F32)


def x_of(x):
    return lax.rem(x + 2 * NX, NX)


def z_of(z):
    return lax.rem(z + 2 * NZ, NZ)


def dp_of(x, z):
    return x_of(x) * NZ + z_of(z)


def remote(src, dst, send, recv, device):
    return pltpu.make_async_remote_copy(
        src_ref=src, dst_ref=dst, send_sem=send, recv_sem=recv, device_id=device, device_id_type=MESH
    )


def arrived(dst, sem):
    pltpu.make_async_copy(dst, dst, sem).wait()


def body_kernel(
    sections, doc_ref, lang_ref, temper_ref, acts_hbm, cot_hbm, w_ref, out_ref,
    x_ref, cot_ref, wf, hb, dy, dx, inv_ref, qkvf, qkvb, kpad, qpad, prob, probb, att, attb, acc, dqkv,
    hbx, obx, dyx, dqx, xs, xr, tot, near_s, near_r, far_s, far_r,
    load_sem, own_sem, gz_s, gz_r, gx_s, gx_r, ch_s, ch_r, hx_s, hx_r, ox_s, ox_r, yx_s, yx_r, qx_s, qx_r, sx_s, sx_r,
    sn_s, sn_r, sf_s, sf_r,
):
    s = lax.axis_index("section")
    me = lax.axis_index("dp")
    x, z = me // NZ, lax.rem(me, NZ)
    toks, depth = x_ref.shape
    part = w_ref.shape[0]
    blocks = toks // ROWS
    wide = depth // NX

    loads = [
        pltpu.make_async_copy(acts_hbm.at[0], x_ref, load_sem.at[0]),
        pltpu.make_async_copy(cot_hbm, cot_ref, load_sem.at[1]),
        pltpu.make_async_copy(w_ref, wf.at[x, z], own_sem),
    ]
    for copy in loads:
        copy.start()
    barrier = pltpu.get_barrier_semaphore()
    reach = FAR + tuple(d for d, start, size in NEAR)
    others = [{"dp": dp_of(x, z + d)} for d in sorted({d % NZ for d in reach} | {-d % NZ for d in reach})]
    others += [{"dp": dp_of(x + k, z)} for k in range(1, NX)]
    others += [{"section": lax.rem(s + 1, sections)}, {"section": lax.rem(s + sections - 1, sections)}]
    for other in others:
        pl.semaphore_signal(barrier, inc=1, device_id=other, device_id_type=MESH)
    pl.semaphore_wait(barrier, len(others))

    sends = []

    def go(copy):
        copy.start()
        sends.append(copy)

    quarter = part // 4
    everyone = pl.ds(0, part)
    near_rows = [pl.ds(start * quarter, size * quarter) for d, start, size in NEAR]

    def put(src, ahead, rows, index, d, send):
        dst = wf.at[x, z_of(z + ahead), rows]
        src = dst if src is None else src.at[rows]
        remote(src, dst, gz_s.at[send], gz_r.at[index], {"dp": dp_of(x, z + d)}).start()
        return (ahead - d, rows, gz_r.at[index])

    def across(src, ahead, rows):
        dst = wf.at[x, z_of(z + ahead), rows]
        src = dst if src is None else src.at[rows]
        for k in TURN:
            remote(src, dst, gx_s.at[k - 1], gx_r.at[k - 1], {"dp": dp_of(x + k, z)}).start()

    n_far, n_near = len(FAR), len(NEAR)
    far_in = [put(w_ref, 0, everyone, i, d, 0) for i, d in enumerate(FAR)]
    across(w_ref, 0, everyone)
    near_in = [put(w_ref, 0, near_rows[i], n_far + i, d, 1 + i) for i, (d, start, size) in enumerate(NEAR)]

    def normalise(i, carry):
        rows = pl.ds(pl.multiple_of(i * ROWS, ROWS), ROWS)
        wide_x = x_ref[rows, :].astype(F32)
        inv = lax.rsqrt(jnp.sum(wide_x * wide_x, axis=1, keepdims=True) / depth + 1e-05)
        inv_ref[rows, :] = inv
        for xx in range(NX):
            hb[xx, rows, :] = (wide_x[:, xx * wide : (xx + 1) * wide] * inv).astype(BF16)
        return carry

    loads[0].wait()
    lax.fori_loop(0, blocks, normalise, 0)
    loads[1].wait()
    loads[2].wait()

    for j, (ahead, rows, recv) in enumerate(far_in):
        arrived(wf.at[x, z_of(z + ahead), rows], recv)
        for i, (d, start, size) in enumerate(NEAR):
            near_in.append(put(None, ahead, near_rows[i], n_far + (j + 1) * n_near + i, d, 1 + i))
        across(None, ahead, rows)
    for ahead, rows, recv in near_in:
        arrived(wf.at[x, z_of(z + ahead), rows], recv)
        across(None, ahead, rows)

    @pl.when(s == sections - 1)
    def _():
        weights = [temper_ref[lang_ref[doc_ref[i]]] for i in range(2)]

        def temper_rows(i, carry):
            rows = pl.ds(pl.multiple_of(i * ROWS, ROWS), ROWS)
            index = i * ROWS + lax.broadcasted_iota(jnp.int32, (ROWS, 1), 0)
            level = jnp.where(index < toks // 2, weights[0], weights[1])
            for xx in range(NX):
                dy[xx, rows, :] = (cot_ref[rows, pl.ds(xx * wide, wide)].astype(F32) * level).astype(BF16)
            return carry

        lax.fori_loop(0, blocks, temper_rows, 0)

    for k in TURN:
        arrived(wf.at[x_of(x - k)], gx_r.at[k - 1])

    def column_of(k):
        return x_of(x + k)

    peers = [(k - 1, k, {"dp": dp_of(x + k, z)}) for k in TURN]
    share_hb = [remote(hb.at[column_of(k)], hbx.at[j], hx_s.at[j], hx_r.at[j], device) for j, k, device in peers]

    @pl.when(s < sections - LATE)
    def _():
        for copy in share_hb:
            copy.start()

    def project(left, rows):
        total = None
        for xx in range(NX):
            term = mm(left[xx, rows, :], wf[xx].reshape(wide, WIDE))
            total = term if total is None else total + term
        return total

    lane = lax.broadcasted_iota(jnp.int32, (1, WIDE), 1)
    is_q, is_k = lane < DH, (lane >= DH) & (lane < 2 * DH)
    is_v = (lane >= 2 * DH) & (lane < 3 * DH)
    scale = DH ** (-0.5)

    everything = pl.ds(0, toks)
    qkv = project(hb, everything)
    qkvf[...] = qkv
    low = qkv.astype(BF16)
    qkvb[...] = low
    keys = jnp.where(is_q, pltpu.roll(qkv, WIDE - DH, 1), 0.0).astype(BF16)
    kpad[...] = keys
    qpad[...] = jnp.where(is_k, pltpu.roll(qkv, DH, 1), 0.0).astype(BF16)
    queries = jnp.where(is_q, qkv, 0.0).astype(BF16)
    row = lax.broadcasted_iota(jnp.int32, (toks, toks), 0)
    col = lax.broadcasted_iota(jnp.int32, (toks, toks), 1)
    joined = (jnp.full((toks, toks), doc_ref[0], jnp.int32) == jnp.full((toks, toks), doc_ref[1], jnp.int32))
    allowed = (col <= row) & (joined | ((row < toks // 2) == (col < toks // 2)))
    terms = jnp.where(allowed, jnp.exp(mm(queries, keys, NT) * scale), 0.0)
    probs = terms / jnp.sum(terms, axis=1, keepdims=True)
    prob[...] = probs
    probb[...] = probs.astype(BF16)
    attended = jnp.where(is_v, mm(probs.astype(BF16), low), 0.0)
    att[...] = attended
    attb[...] = pltpu.roll(attended, DH, 1).astype(BF16)
    acc[...] = jnp.zeros_like(acc)
    share_ob = [remote(attb, obx.at[j], ox_s.at[j], ox_r.at[j], device) for j, k, device in peers]

    @pl.when(s < sections - LATE)
    def _():
        for copy in share_ob:
            copy.start()

    def share_dy(block):
        rows = pl.ds(pl.multiple_of(block * ROWS, ROWS), ROWS)
        return [
            remote(dy.at[column_of(k), rows], dyx.at[j, rows], yx_s.at[j], yx_r.at[j], device)
            for j, k, device in peers
        ]

    def share_dq(block):
        rows = pl.ds(pl.multiple_of(block * ROWS, ROWS), ROWS)
        return [
            remote(dqkv.at[rows], dqx.at[j, rows], qx_s.at[j], qx_r.at[j], device)
            for j, k, device in peers
        ]

    group = NX // SPLIT

    def pass_down(block, i):
        at = (pl.ds(i * group, group), pl.ds(pl.multiple_of(block * ROWS, ROWS), ROWS))
        return remote(dx.at[at], dy.at[at], ch_s.at[i], ch_r.at[i, block], {"section": s - 1})

    def chain(i, carry):
        block = blocks - 1 - i
        rows = pl.ds(pl.multiple_of(block * ROWS, ROWS), ROWS)

        projected = None
        for xx in range(NX):

            if xx % group == 0:

                @pl.when(s < sections - 1)
                def _():
                    arrived(dy.at[pl.ds(xx, group), rows], ch_r.at[xx // group, block])

            term = mm(dy[xx, rows, :], wf[xx].reshape(wide, WIDE))
            projected = term if projected is None else projected + term

        @pl.when(s == 0)
        def _():
            for copy in share_dy(block):
                copy.start()

        out_grad = jnp.where(is_v, pltpu.roll(projected, WIDE - DH, 1), 0.0).astype(BF16)
        delta = jnp.sum(out_grad.astype(F32) * att[rows, :], axis=1, keepdims=True)
        prob_grad = mm(out_grad, qkvb[...], NT)
        score_grad = (prob[rows, :] * (prob_grad - delta) * scale).astype(BF16)
        acc[...] += mm(score_grad, qpad[rows, :], TN) + mm(probb[rows, :], out_grad, TN)
        proj_grad = (mm(score_grad, kpad[...]) + acc[rows, :]).astype(BF16)
        dqkv[rows, :] = proj_grad

        @pl.when(s > 0)
        def _():
            inv = inv_ref[rows, :]
            pull = inv * inv * (jnp.sum(proj_grad.astype(F32) * qkvf[rows, :], axis=1, keepdims=True) / depth)
            for xx in range(NX):
                span = pl.ds(xx * wide, wide)
                back = mm(proj_grad, wf[xx].reshape(wide, WIDE), NT)
                dx[xx, rows, :] = (
                    dy[xx, rows, :].astype(F32) + inv * back - x_ref[rows, span].astype(F32) * pull
                ).astype(BF16)
                if (xx + 1) % group == 0:
                    pass_down(block, xx // group).start()

        @pl.when((s > 0) & (s < sections - LATE))
        def _():
            for copy in share_dy(block):
                copy.start()

        @pl.when(s < sections - LATE)
        def _():
            for copy in share_dq(block):
                copy.start()

        return carry

    lax.fori_loop(0, blocks, chain, 0)

    def tile(k):
        return mm(hb[column_of(k)], dqkv[...], TN) + mm(dy[column_of(k)], attb[...], TN)

    @pl.when(s >= sections - LATE)
    def _():
        swaps = []
        for j, k, device in peers:
            xs[j] = tile(k).astype(BF16)
            swaps.append(remote(xs.at[j], xr.at[j], sx_s.at[j], sx_r.at[j], device))
            swaps[-1].start()
        tot[...] = tile(0)
        for i, (j, k, device) in enumerate(peers):
            swaps[i].wait()
            tot[...] += xr[j].astype(F32)

    @pl.when(s < sections - LATE)
    def _():
        tot[...] = tile(0)
        for copy in share_hb + share_ob:
            copy.wait()

        for j, k, device in peers:
            arrived(dyx.at[j], yx_r.at[j])
            arrived(dqx.at[j], qx_r.at[j])
            tot[...] += mm(hbx[j], dqx[j], TN) + mm(dyx[j], obx[j], TN)

    def mine(zz, start=0, size=4):
        first = z_of(zz) * part + start * quarter
        return tot[pl.ds(pl.multiple_of(first, quarter), size * quarter), :]

    ends = (0,) + FAR
    hops = []
    for i, (d, start, size) in enumerate(NEAR):
        rows = pl.ds(0, size * quarter)
        for j, a in enumerate(ends):
            near_s[i, j, rows, :] = mine(z + d + a, start, size).astype(BF16)
        hops.append(
            remote(near_s.at[i, :, rows], near_r.at[i, :, rows], sn_s.at[i], sn_r.at[i], {"dp": dp_of(x, z + d)})
        )
        go(hops[i])
    for copy in hops:
        copy.wait_recv()

    def gathered(j):
        halves = []
        for h in (0, 2):
            total = mine(z + ends[j], h, 2)
            for i, (d, start, size) in enumerate(NEAR):
                if start <= h < start + size:
                    total = total + near_r[i, j, pl.ds((h - start) * quarter, 2 * quarter), :].astype(F32)
            halves.append(total)
        return jnp.concatenate(halves, axis=0)

    hops = []
    for j, a in enumerate(FAR):
        far_s[j] = gathered(j + 1).astype(BF16)
        hops.append(remote(far_s.at[j], far_r.at[j], sf_s.at[j], sf_r.at[j], {"dp": dp_of(x, z + a)}))
        go(hops[j])
    total = gathered(0)
    for j, copy in enumerate(hops):
        copy.wait_recv()
        total = total + far_r[j].astype(F32)
    out_ref[...] = total
    for copy in sends:
        copy.wait_send()
    for k in TURN:
        arrived(wf.at[x], gx_s.at[k - 1])
    arrived(wf.at[0, pl.ds(0, n_far)], gz_s.at[0])
    for i in range(n_near):
        arrived(wf.at[0, pl.ds(0, n_far + 1), near_rows[i]], gz_s.at[1 + i])

    @pl.when(s < sections - LATE)
    def _():
        for j, k, device in peers:
            arrived(dyx.at[j], yx_s.at[j])
            arrived(dqx.at[j], qx_s.at[j])

    @pl.when(s > 0)
    def _():
        for i in range(SPLIT):
            arrived(dx.at[pl.ds(i * group, group)], ch_s.at[i])


def body(acts, cotangent, weights, doc_ids, lang_ids, temper):
    sections = lax.axis_size("section")
    toks, depth = cotangent.shape
    part = weights.shape[1]
    near, far = len(NEAR), len(FAR)
    slots = far + (1 + far) * near
    wide = depth // NX
    blocks = toks // ROWS
    dma = pltpu.SemaphoreType.DMA
    vmem = pltpu.VMEM
    smem = pl.BlockSpec(memory_space=pltpu.SMEM)
    hbm = pl.BlockSpec(memory_space=pl.ANY)
    grads = pl.pallas_call(
        partial(body_kernel, sections),
        out_shape=jax.ShapeDtypeStruct((part, WIDE), F32),
        in_specs=[smem, smem, smem, hbm, hbm, pl.BlockSpec(memory_space=pltpu.VMEM)],
        out_specs=pl.BlockSpec(memory_space=pltpu.VMEM),
        scratch_shapes=[
            vmem((toks, depth), BF16),
            vmem((toks, depth), BF16),
            vmem((NX, NZ, part, WIDE), BF16),
            vmem((NX, toks, wide), BF16),
            vmem((NX, toks, wide), BF16),
            vmem((NX, toks, wide), BF16),
            vmem((toks, 1), F32),
            vmem((toks, WIDE), F32),
            vmem((toks, WIDE), BF16),
            vmem((toks, WIDE), BF16),
            vmem((toks, WIDE), BF16),
            vmem((toks, toks), F32),
            vmem((toks, toks), BF16),
            vmem((toks, WIDE), F32),
            vmem((toks, WIDE), BF16),
            vmem((toks, WIDE), F32),
            vmem((toks, WIDE), BF16),
            vmem((NX - 1, toks, wide), BF16),
            vmem((NX - 1, toks, WIDE), BF16),
            vmem((NX - 1, toks, wide), BF16),
            vmem((NX - 1, toks, WIDE), BF16),
            vmem((NX - 1, wide, WIDE), BF16),
            vmem((NX - 1, wide, WIDE), BF16),
            vmem((wide, WIDE), F32),
            vmem((near, far + 1, part, WIDE), BF16),
            vmem((near, far + 1, part, WIDE), BF16),
            vmem((far, part, WIDE), BF16),
            vmem((far, part, WIDE), BF16),
            dma((2,)),
            dma,
            dma((1 + near,)),
            dma((slots,)),
            dma((NX - 1,)),
            dma((NX - 1,)),
            dma((SPLIT,)),
            dma((SPLIT, blocks)),
            dma((NX - 1,)),
            dma((NX - 1,)),
            dma((NX - 1,)),
            dma((NX - 1,)),
            dma((NX - 1,)),
            dma((NX - 1,)),
            dma((NX - 1,)),
            dma((NX - 1,)),
            dma((NX - 1,)),
            dma((NX - 1,)),
            dma((near,)),
            dma((near,)),
            dma((far,)),
            dma((far,)),
        ],
        compiler_params=pltpu.CompilerParams(collective_id=0, has_side_effects=True, vmem_limit_bytes=VMEM_LIMIT),
        name="layer_chain",
    )(doc_ids, lang_ids, temper, acts, cotangent, weights[0])
    return grads[None]


def solution(mesh):
    return jax.shard_map(
        body,
        mesh=mesh,
        in_specs=(
            P("section", "dp", None),
            P("dp", None),
            P("section", "dp", None),
            P("dp"),
            P("dp"),
            P(),
        ),
        out_specs=P("section", "dp", None),
        check_vma=False,
    )
```

```python
from functools import partial

import jax
import jax.numpy as jnp
from jax import lax
from jax.experimental import pallas as pl
from jax.experimental.pallas import tpu as pltpu
from jax.sharding import PartitionSpec as P

DH = 64
WIDE = 4 * DH
MESH = pl.DeviceIdType.MESH
NX = 4
NZ = 16
ROWS = 32
FAR = (8, 4, -4)
NEAR = ((2, 0, 2), (-2, 2, 2), (1, 0, 4), (-1, 0, 4))
TURN = (2, 1, 3)
LATE = 2
SPLIT = 4
VMEM_LIMIT = 58 << 20
F32 = jnp.float32
BF16 = jnp.bfloat16
NT = (((1,), (1,)), ((), ()))
TN = (((0,), (0,)), ((), ()))


def mm(a, b, dims=(((1,), (0,)), ((), ()))):
    return lax.dot_general(a, b, dims, preferred_element_type=F32)


def x_of(x):
    return lax.rem(x + 2 * NX, NX)


def z_of(z):
    return lax.rem(z + 2 * NZ, NZ)


def dp_of(x, z):
    return x_of(x) * NZ + z_of(z)


def remote(src, dst, send, recv, device):
    return pltpu.make_async_remote_copy(
        src_ref=src, dst_ref=dst, send_sem=send, recv_sem=recv, device_id=device, device_id_type=MESH
    )


def arrived(dst, sem):
    pltpu.make_async_copy(dst, dst, sem).wait()


def body_kernel(
    sections, doc_ref, lang_ref, temper_ref, acts_hbm, cot_hbm, w_ref, out_ref,
    x_ref, cot_ref, wf, hb, dy, dx, inv_ref, qkvf, qkvb, kpad, qpad, prob, probb, att, attb, acc, dqkv,
    hbx, left, right, ps, pr, dqx, xs, xr, tot, near_s, near_r, far_s, far_r,
    load_sem, own_sem, gz_s, gz_r, gx_s, gx_r, ch_s, ch_r, hx_s, hx_r, yx_s, yx_r, qx_s, qx_r, sx_s, sx_r,
    sn_s, sn_r, sf_s, sf_r,
):
    s = lax.axis_index("section")
    me = lax.axis_index("dp")
    x, z = me // NZ, lax.rem(me, NZ)
    toks, depth = x_ref.shape
    part = w_ref.shape[0]
    blocks = toks // ROWS
    wide = depth // NX

    loads = [
        pltpu.make_async_copy(acts_hbm.at[0], x_ref, load_sem.at[0]),
        pltpu.make_async_copy(cot_hbm, cot_ref, load_sem.at[1]),
        pltpu.make_async_copy(w_ref, wf.at[x, z], own_sem),
    ]
    for copy in loads:
        copy.start()
    barrier = pltpu.get_barrier_semaphore()
    reach = FAR + tuple(d for d, start, size in NEAR)
    others = [{"dp": dp_of(x, z + d)} for d in sorted({d % NZ for d in reach} | {-d % NZ for d in reach})]
    others += [{"dp": dp_of(x + k, z)} for k in range(1, NX)]
    others += [{"section": lax.rem(s + 1, sections)}, {"section": lax.rem(s + sections - 1, sections)}]
    for other in others:
        pl.semaphore_signal(barrier, inc=1, device_id=other, device_id_type=MESH)
    pl.semaphore_wait(barrier, len(others))

    sends = []

    def go(copy):
        copy.start()
        sends.append(copy)

    quarter = part // 4
    everyone = pl.ds(0, part)
    near_rows = [pl.ds(start * quarter, size * quarter) for d, start, size in NEAR]

    def put(src, ahead, rows, index, d, send):
        dst = wf.at[x, z_of(z + ahead), rows]
        src = dst if src is None else src.at[rows]
        remote(src, dst, gz_s.at[send], gz_r.at[index], {"dp": dp_of(x, z + d)}).start()
        return (ahead - d, rows, gz_r.at[index])

    def across(src, ahead, rows):
        dst = wf.at[x, z_of(z + ahead), rows]
        src = dst if src is None else src.at[rows]
        for k in TURN:
            remote(src, dst, gx_s.at[k - 1], gx_r.at[k - 1], {"dp": dp_of(x + k, z)}).start()

    n_far, n_near = len(FAR), len(NEAR)
    far_in = [put(w_ref, 0, everyone, i, d, 0) for i, d in enumerate(FAR)]
    across(w_ref, 0, everyone)
    near_in = [put(w_ref, 0, near_rows[i], n_far + i, d, 1 + i) for i, (d, start, size) in enumerate(NEAR)]

    def normalise(i, carry):
        rows = pl.ds(pl.multiple_of(i * ROWS, ROWS), ROWS)
        wide_x = x_ref[rows, :].astype(F32)
        inv = lax.rsqrt(jnp.sum(wide_x * wide_x, axis=1, keepdims=True) / depth + 1e-05)
        inv_ref[rows, :] = inv
        for xx in range(NX):
            hb[xx, rows, :] = (wide_x[:, xx * wide : (xx + 1) * wide] * inv).astype(BF16)
        return carry

    loads[0].wait()
    lax.fori_loop(0, blocks, normalise, 0)
    loads[1].wait()
    loads[2].wait()

    for j, (ahead, rows, recv) in enumerate(far_in):
        arrived(wf.at[x, z_of(z + ahead), rows], recv)
        for i, (d, start, size) in enumerate(NEAR):
            near_in.append(put(None, ahead, near_rows[i], n_far + (j + 1) * n_near + i, d, 1 + i))
        across(None, ahead, rows)
    for ahead, rows, recv in near_in:
        arrived(wf.at[x, z_of(z + ahead), rows], recv)
        across(None, ahead, rows)

    @pl.when(s == sections - 1)
    def _():
        weights = [temper_ref[lang_ref[doc_ref[i]]] for i in range(2)]

        def temper_rows(i, carry):
            rows = pl.ds(pl.multiple_of(i * ROWS, ROWS), ROWS)
            index = i * ROWS + lax.broadcasted_iota(jnp.int32, (ROWS, 1), 0)
            level = jnp.where(index < toks // 2, weights[0], weights[1])
            for xx in range(NX):
                dy[xx, rows, :] = (cot_ref[rows, pl.ds(xx * wide, wide)].astype(F32) * level).astype(BF16)
            return carry

        lax.fori_loop(0, blocks, temper_rows, 0)

    for k in TURN:
        arrived(wf.at[x_of(x - k)], gx_r.at[k - 1])

    def column_of(k):
        return x_of(x + k)

    peers = [(k - 1, k, {"dp": dp_of(x + k, z)}) for k in TURN]
    share_hb = [remote(hb.at[column_of(k)], hbx.at[j], hx_s.at[j], hx_r.at[j], device) for j, k, device in peers]

    @pl.when(s < sections - LATE)
    def _():
        for copy in share_hb:
            copy.start()

    def project(left, rows):
        total = None
        for xx in range(NX):
            term = mm(left[xx, rows, :], wf[xx].reshape(wide, WIDE))
            total = term if total is None else total + term
        return total

    lane = lax.broadcasted_iota(jnp.int32, (1, WIDE), 1)
    is_q, is_k = lane < DH, (lane >= DH) & (lane < 2 * DH)
    is_o = lane >= 3 * DH
    is_v = (lane >= 2 * DH) & (lane < 3 * DH)
    scale = DH ** (-0.5)

    everything = pl.ds(0, toks)
    qkv = project(hb, everything)
    qkvf[...] = qkv
    low = qkv.astype(BF16)
    qkvb[...] = low
    keys = jnp.where(is_q, pltpu.roll(qkv, WIDE - DH, 1), 0.0).astype(BF16)
    kpad[...] = keys
    qpad[...] = jnp.where(is_k, pltpu.roll(qkv, DH, 1), 0.0).astype(BF16)
    queries = jnp.where(is_q, qkv, 0.0).astype(BF16)
    row = lax.broadcasted_iota(jnp.int32, (toks, toks), 0)
    col = lax.broadcasted_iota(jnp.int32, (toks, toks), 1)
    joined = (jnp.full((toks, toks), doc_ref[0], jnp.int32) == jnp.full((toks, toks), doc_ref[1], jnp.int32))
    allowed = (col <= row) & (joined | ((row < toks // 2) == (col < toks // 2)))
    terms = jnp.where(allowed, jnp.exp(mm(queries, keys, NT) * scale), 0.0)
    probs = terms / jnp.sum(terms, axis=1, keepdims=True)
    prob[...] = probs
    probb[...] = probs.astype(BF16)
    attended = jnp.where(is_v, mm(probs.astype(BF16), low), 0.0)
    att[...] = attended
    attb[...] = pltpu.roll(attended, DH, 1).astype(BF16)
    acc[...] = jnp.zeros_like(acc)
    pair = pltpu.roll(attended[:, 2 * DH :], DH, 1)
    right[...] = pair.astype(BF16)
    left[...] = attended[:, 2 * DH :].astype(BF16)

    def share_dq(block):
        rows = pl.ds(pl.multiple_of(block * ROWS, ROWS), ROWS)
        return [
            remote(dqkv.at[rows], dqx.at[j, rows], qx_s.at[j], qx_r.at[j], device)
            for j, k, device in peers
        ]

    group = NX // SPLIT

    def pass_down(block, i):
        at = (pl.ds(i * group, group), pl.ds(pl.multiple_of(block * ROWS, ROWS), ROWS))
        return remote(dx.at[at], dy.at[at], ch_s.at[i], ch_r.at[i, block], {"section": s - 1})

    def chain(i, carry):
        block = blocks - 1 - i
        rows = pl.ds(pl.multiple_of(block * ROWS, ROWS), ROWS)

        projected = None
        for xx in range(NX):

            if xx % group == 0:

                @pl.when(s < sections - 1)
                def _():
                    arrived(dy.at[pl.ds(xx, group), rows], ch_r.at[xx // group, block])

            term = mm(dy[xx, rows, :], wf[xx].reshape(wide, WIDE))
            projected = term if projected is None else projected + term

        out_grad = jnp.where(is_v, pltpu.roll(projected, WIDE - DH, 1), 0.0).astype(BF16)
        delta = jnp.sum(out_grad.astype(F32) * att[rows, :], axis=1, keepdims=True)
        prob_grad = mm(out_grad, qkvb[...], NT)
        score_grad = (prob[rows, :] * (prob_grad - delta) * scale).astype(BF16)
        acc[...] += mm(score_grad, qpad[rows, :], TN) + mm(probb[rows, :], out_grad, TN)
        proj_grad = (mm(score_grad, kpad[...]) + acc[rows, :]).astype(BF16)
        dqkv[rows, :] = proj_grad

        @pl.when(s > 0)
        def _():
            inv = inv_ref[rows, :]
            pull = inv * inv * (jnp.sum(proj_grad.astype(F32) * qkvf[rows, :], axis=1, keepdims=True) / depth)
            for xx in range(NX):
                span = pl.ds(xx * wide, wide)
                back = mm(proj_grad, wf[xx].reshape(wide, WIDE), NT)
                dx[xx, rows, :] = (
                    dy[xx, rows, :].astype(F32) + inv * back - x_ref[rows, span].astype(F32) * pull
                ).astype(BF16)
                if (xx + 1) % group == 0:
                    pass_down(block, xx // group).start()

        @pl.when(s < sections - LATE)
        def _():
            for copy in share_dq(block):
                copy.start()

        return carry

    lax.fori_loop(0, blocks, chain, 0)

    def tile(k):
        return mm(hb[column_of(k)], dqkv[...], TN) + mm(dy[column_of(k)], attb[...], TN)

    @pl.when(s >= sections - LATE)
    def _():
        swaps = []
        for j, k, device in peers:
            xs[j] = tile(k).astype(BF16)
            swaps.append(remote(xs.at[j], xr.at[j], sx_s.at[j], sx_r.at[j], device))
            swaps[-1].start()
        tot[...] = tile(0)
        for i, (j, k, device) in enumerate(peers):
            swaps[i].wait()
            tot[...] += xr[j].astype(F32)

    @pl.when(s < sections - LATE)
    def _():
        swaps = []
        half = wide // 2
        for j, k, device in peers:
            piece = mm(dy[column_of(k), :, pl.ds(0, half)], left[...], TN)
            piece += mm(dy[column_of(k), :, pl.ds(half, half)], right[...], TN)
            ps[j] = piece.astype(BF16)
            swaps.append(remote(ps.at[j], pr.at[j], yx_s.at[j], yx_r.at[j], device))
            swaps[-1].start()
        tot[...] = tile(0)
        for copy in share_hb:
            copy.wait()

        for j, k, device in peers:
            arrived(dqx.at[j], qx_r.at[j])
            tot[...] += mm(hbx[j], dqx[j], TN)
        summed = None
        for copy, (j, k, device) in zip(swaps, peers):
            copy.wait()
            term = pr[j].astype(F32)
            summed = term if summed is None else summed + term
        spread = jnp.concatenate([jnp.zeros_like(summed), summed], axis=1)
        tot[pl.ds(0, half), :] += jnp.where(is_o, pltpu.roll(spread, DH, 1), 0.0)
        tot[pl.ds(half, half), :] += jnp.where(is_o, spread, 0.0)

    def mine(zz, start=0, size=4):
        first = z_of(zz) * part + start * quarter
        return tot[pl.ds(pl.multiple_of(first, quarter), size * quarter), :]

    ends = (0,) + FAR
    hops = []
    for i, (d, start, size) in enumerate(NEAR):
        rows = pl.ds(0, size * quarter)
        for j, a in enumerate(ends):
            near_s[i, j, rows, :] = mine(z + d + a, start, size).astype(BF16)
        hops.append(
            remote(near_s.at[i, :, rows], near_r.at[i, :, rows], sn_s.at[i], sn_r.at[i], {"dp": dp_of(x, z + d)})
        )
        go(hops[i])
    for copy in hops:
        copy.wait_recv()

    def gathered(j):
        halves = []
        for h in (0, 2):
            total = mine(z + ends[j], h, 2)
            for i, (d, start, size) in enumerate(NEAR):
                if start <= h < start + size:
                    total = total + near_r[i, j, pl.ds((h - start) * quarter, 2 * quarter), :].astype(F32)
            halves.append(total)
        return jnp.concatenate(halves, axis=0)

    hops = []
    for j, a in enumerate(FAR):
        far_s[j] = gathered(j + 1).astype(BF16)
        hops.append(remote(far_s.at[j], far_r.at[j], sf_s.at[j], sf_r.at[j], {"dp": dp_of(x, z + a)}))
        go(hops[j])
    total = gathered(0)
    for j, copy in enumerate(hops):
        copy.wait_recv()
        total = total + far_r[j].astype(F32)
    out_ref[...] = total
    for copy in sends:
        copy.wait_send()
    for k in TURN:
        arrived(wf.at[x], gx_s.at[k - 1])
    arrived(wf.at[0, pl.ds(0, n_far)], gz_s.at[0])
    for i in range(n_near):
        arrived(wf.at[0, pl.ds(0, n_far + 1), near_rows[i]], gz_s.at[1 + i])

    @pl.when(s < sections - LATE)
    def _():
        for j, k, device in peers:
            arrived(dqx.at[j], qx_s.at[j])

    @pl.when(s > 0)
    def _():
        for i in range(SPLIT):
            arrived(dx.at[pl.ds(i * group, group)], ch_s.at[i])


def body(acts, cotangent, weights, doc_ids, lang_ids, temper):
    sections = lax.axis_size("section")
    toks, depth = cotangent.shape
    part = weights.shape[1]
    near, far = len(NEAR), len(FAR)
    slots = far + (1 + far) * near
    wide = depth // NX
    blocks = toks // ROWS
    dma = pltpu.SemaphoreType.DMA
    vmem = pltpu.VMEM
    smem = pl.BlockSpec(memory_space=pltpu.SMEM)
    hbm = pl.BlockSpec(memory_space=pl.ANY)
    grads = pl.pallas_call(
        partial(body_kernel, sections),
        out_shape=jax.ShapeDtypeStruct((part, WIDE), F32),
        in_specs=[smem, smem, smem, hbm, hbm, pl.BlockSpec(memory_space=pltpu.VMEM)],
        out_specs=pl.BlockSpec(memory_space=pltpu.VMEM),
        scratch_shapes=[
            vmem((toks, depth), BF16),
            vmem((toks, depth), BF16),
            vmem((NX, NZ, part, WIDE), BF16),
            vmem((NX, toks, wide), BF16),
            vmem((NX, toks, wide), BF16),
            vmem((NX, toks, wide), BF16),
            vmem((toks, 1), F32),
            vmem((toks, WIDE), F32),
            vmem((toks, WIDE), BF16),
            vmem((toks, WIDE), BF16),
            vmem((toks, WIDE), BF16),
            vmem((toks, toks), F32),
            vmem((toks, toks), BF16),
            vmem((toks, WIDE), F32),
            vmem((toks, WIDE), BF16),
            vmem((toks, WIDE), F32),
            vmem((toks, WIDE), BF16),
            vmem((NX - 1, toks, wide), BF16),
            vmem((toks, 2 * DH), BF16),
            vmem((toks, 2 * DH), BF16),
            vmem((NX - 1, wide // 2, 2 * DH), BF16),
            vmem((NX - 1, wide // 2, 2 * DH), BF16),
            vmem((NX - 1, toks, WIDE), BF16),
            vmem((NX - 1, wide, WIDE), BF16),
            vmem((NX - 1, wide, WIDE), BF16),
            vmem((wide, WIDE), F32),
            vmem((near, far + 1, part, WIDE), BF16),
            vmem((near, far + 1, part, WIDE), BF16),
            vmem((far, part, WIDE), BF16),
            vmem((far, part, WIDE), BF16),
            dma((2,)),
            dma,
            dma((1 + near,)),
            dma((slots,)),
            dma((NX - 1,)),
            dma((NX - 1,)),
            dma((SPLIT,)),
            dma((SPLIT, blocks)),
            dma((NX - 1,)),
            dma((NX - 1,)),
            dma((NX - 1,)),
            dma((NX - 1,)),
            dma((NX - 1,)),
            dma((NX - 1,)),
            dma((NX - 1,)),
            dma((NX - 1,)),
            dma((near,)),
            dma((near,)),
            dma((far,)),
            dma((far,)),
        ],
        compiler_params=pltpu.CompilerParams(collective_id=0, has_side_effects=True, vmem_limit_bytes=VMEM_LIMIT),
        name="layer_chain",
    )(doc_ids, lang_ids, temper, acts, cotangent, weights[0])
    return grads[None]


def solution(mesh):
    return jax.shard_map(
        body,
        mesh=mesh,
        in_specs=(
            P("section", "dp", None),
            P("dp", None),
            P("section", "dp", None),
            P("dp"),
            P("dp"),
            P(),
        ),
        out_specs=P("section", "dp", None),
        check_vma=False,
    )
```
